32 devices in a mesh: groups: 2 (over x), panel: 16 (over z, y, core).
Axes of the slice: x: 2, y: 2, z: 4, core: 2. Of those that a mesh axis runs over, the one named last changes fastest.
Arguments:
- eig_vectors: bfloat16 [5120, 1024], P(('groups', 'panel')), parts along dimension 0, may hold values from -0.1875 to 0.1875
- eig_values: bfloat16 [5120], P(('groups', 'panel')), parts along dimension 0, may hold values from 0.19921875 to 5
- eig_count: int32 [16], P('groups'), parts along dimension 0, may hold values from 128 to 512, as said below
- snp_count: int32 [16], P('groups'), parts along dimension 0, may hold values from 512 to 1024
- zscores: bfloat16 [32, 8, 1024, 128], P(('groups', 'panel')), parts along dimension 0, may hold values from -6 to 6
- samples: bfloat16 [4096], P('groups'), parts along dimension 0, may hold values from 20 to 160
Outputs:
- covariance: float32 [9, 32, 8, 128, 128], P(None, ('groups', 'panel')), parts along dimension 1
The draws below stay inside these ranges and needn't reach their ends.
There are 2 independent parts, one for each index of `groups`. The reference program is written for one: setup_inputs(seed, part) draws one part's arguments, and reference() takes and returns one part's arrays. A program takes and returns all parts, laid end to end along the dimension named above; each array names one. Nothing has to cross between parts.
Inputs may be any that keep to these rules, and one draw needn't show every extreme that they name: `eig_count`: blocks 2m and 2m+1 hold 640 eigenvectors together, so every block group holds 2560; some block holds exactly 512.
All inputs are finite; a program needn't handle non-finite values.
Results may differ from the reference program's by a relative error of at most 0.0045.
Values may be sent and summed in bfloat16 or wider, within the bound.
A program may use at most 64 MiB of HBM per device.

```python
import math
import jax
import jax.numpy as jnp
from jax import lax

PW = 128
MB = 1024
KMAX = 512
KMEAN = 320
BLOCKS = 8
ROUNDS = 8
BG = 1
NP = 16
TRAITS = 2048
BPG = 8
GROUP_ROWS = 2560
EIGS = 2560
EIG_DEV = 160
N_PANEL = 16


def draw_eig_count(key, part):
    pair_count = BLOCKS // 2
    spread = KMAX - KMEAN
    key_left, key_right = jax.random.split(jax.random.fold_in(key, 17))
    offset_draw = jax.random.randint(key_left, (pair_count,), -spread, spread + 1)
    forced = jax.random.randint(key_right, (), 0, pair_count)
    offset_draw = jnp.where(jnp.arange(pair_count) == forced, spread, offset_draw)
    counts = jnp.stack([KMEAN + offset_draw, KMEAN - offset_draw], axis=1).reshape(BLOCKS)
    return counts.astype(jnp.int32)


def with_ends(result, stream_key, low, largest):
    longest = result.shape.index(max(result.shape))
    spots = []
    for shift in (0, 1):
        where = [jax.random.randint(jax.random.fold_in(stream_key, axis), (), 0, length) for axis, length in enumerate(result.shape)]
        where[longest] = (where[longest] + shift) % result.shape[longest]
        spots.append(tuple(where))
    return result.at[spots[0]].set(low).at[spots[1]].set(largest)


def steps_of(rng, extent, cuts, least, high):
    gain, own = 1.0, jax.random.fold_in(rng, 6)
    for axis_at, shards_of in cuts:
        draws = jnp.exp(jax.random.uniform(jax.random.fold_in(own, axis_at), (shards_of,), jnp.float32, least / len(cuts), high / len(cuts)))
        gain = gain * jnp.repeat(draws, extent[axis_at] // shards_of).reshape([-1 if axis == axis_at else 1 for axis in range(len(extent))])
    return gain


def noise(rng, extent, scale, reach, cuts=(), kind=jnp.bfloat16):
    entries = jax.random.normal(rng, extent, jnp.float32) * scale
    if len(cuts) > 0:
        entries = steps_of(rng, extent, cuts, -0.22, 0.18) * entries
    return jnp.clip(entries, min=-reach, max=reach).astype(kind)


def setup_inputs(seed: int = 0, part: int = 0) -> dict:
    key_of = jax.random.split(jax.random.key(seed), 7)
    part_keys = jax.random.split(jax.random.fold_in(key_of[6], part), 7)
    eig_vectors = noise(part_keys[0], (EIGS, MB), MB ** -0.5, 0.1875, ((0, 16),))
    eig_values = jnp.clip(jnp.exp(math.log(5.0) - 3.2227897 * jax.random.uniform(part_keys[1], (EIGS,), jnp.float32) ** steps_of(part_keys[1], (EIGS,), ((0, 16),), -0.2, 0.2)), 0.19921875, 5.0).astype(jnp.bfloat16)
    eig_count = draw_eig_count(jax.random.fold_in(jax.random.fold_in(key_of[6], part), 71), part)
    snp_count = with_ends(jax.random.randint(part_keys[3], (BLOCKS,), MB // 2, MB + 1), jax.random.fold_in(part_keys[3], 1), MB // 2, MB).astype(jnp.int32)
    zscores = noise(part_keys[4], (N_PANEL, BPG, MB, PW), 1.0, 6.0, ((0, 16),))
    samples = jnp.clip(jnp.exp(jax.random.uniform(part_keys[5], (TRAITS,), jnp.float32, math.log(20.0), math.log(160.0))), 20.0, 160.0).astype(jnp.bfloat16)
    return dict(eig_vectors=eig_vectors, eig_values=eig_values, eig_count=eig_count, snp_count=snp_count, zscores=zscores, samples=samples)


def project_blocks(vectors, counts, snps, scores):
    offsets = (jnp.cumsum(counts) - counts).astype(jnp.int32)
    row_total = vectors.shape[0]
    positions = jnp.arange(scores.shape[1], dtype=jnp.int32)
    kept = jnp.arange(KMAX, dtype=jnp.int32)

    def one_block(block_index, projected):
        start_row = offsets[block_index]
        live_count = counts[block_index]
        row_start = jnp.minimum(start_row, row_total - KMAX).astype(jnp.int32)
        eig_rows = lax.dynamic_slice_in_dim(vectors, row_start, KMAX, 0)
        block_scores = lax.dynamic_index_in_dim(scores, block_index, 0, keepdims=False)
        z_masked = jnp.where((positions < snps[block_index])[:, None], block_scores, jnp.zeros_like(block_scores))
        projection = jnp.dot(eig_rows, z_masked, preferred_element_type=jnp.float32).astype(jnp.bfloat16)
        row_index = row_start + kept
        keep_rows = (row_index >= start_row) & (row_index < start_row + live_count)
        previous = lax.dynamic_slice_in_dim(projected, row_start, KMAX, 0)
        merged = jnp.where(keep_rows[:, None], projection, previous)
        return lax.dynamic_update_slice_in_dim(projected, merged, row_start, 0)
    initial = jnp.zeros((row_total, scores.shape[2]), jnp.bfloat16)
    return lax.fori_loop(0, counts.shape[0], one_block, initial)

def reference(eig_vectors, eig_values, eig_count, snp_count, zscores, samples):
    vectors_all = eig_vectors.reshape(NP, BG, EIG_DEV, MB)
    values_all = eig_values.reshape(NP, BG, EIG_DEV)
    scores_all = zscores.reshape(NP, BG, BPG, MB, PW)
    scales = samples.astype(jnp.float32).reshape(NP, PW)
    kept = jnp.arange(KMAX, dtype=jnp.int32)
    group_results = []
    for group_index in range(BG):
        vectors = vectors_all[:, group_index].reshape(GROUP_ROWS, MB)
        values = values_all[:, group_index].reshape(GROUP_ROWS)
        counts = eig_count[group_index * BPG:(group_index + 1) * BPG]
        snps = snp_count[group_index * BPG:(group_index + 1) * BPG]
        scores = jnp.transpose(scores_all[:, group_index], (1, 2, 0, 3)).reshape(BPG, MB, NP * PW)
        projected = project_blocks(vectors, counts, snps, scores)
        weighted = (projected.astype(jnp.float32) / values.astype(jnp.float32)[:, None]).astype(jnp.bfloat16)
        weighted_wide = weighted.astype(jnp.float32).reshape(GROUP_ROWS, NP, PW)
        projected_wide = projected.astype(jnp.float32).reshape(GROUP_ROWS, NP, PW)
        offsets = (jnp.cumsum(counts) - counts).astype(jnp.int32)
        round_results = []
        for round_index in range(ROUNDS + 1):
            partner = jnp.roll(projected_wide, round_index, axis=1)
            partner_scale = jnp.roll(scales, round_index, axis=0)

            def block_gram(block_index):
                start_row = offsets[block_index]
                row_start = jnp.minimum(start_row, GROUP_ROWS - KMAX).astype(jnp.int32)
                row_index = row_start + kept
                keep_rows = (row_index >= start_row) & (row_index < start_row + counts[block_index])
                left_slab = lax.dynamic_slice_in_dim(weighted_wide, row_start, KMAX, 0)
                left_slab = jnp.where(keep_rows[:, None, None], left_slab, jnp.zeros_like(left_slab))
                right_slab = lax.dynamic_slice_in_dim(partner, row_start, KMAX, 0)
                gram = jnp.einsum('kpa,kpc->pac', left_slab, right_slab, precision=lax.Precision.HIGHEST)
                if round_index == 0:
                    gram = gram - counts[block_index].astype(jnp.float32) * jnp.eye(PW, dtype=jnp.float32)[None]
                return gram / jnp.sqrt(scales[:, :, None] * partner_scale[:, None, :])
            grams = lax.map(block_gram, jnp.arange(BPG, dtype=jnp.int32))
            round_results.append(jnp.transpose(grams, (1, 0, 2, 3)))
        group_results.append(jnp.stack(round_results))
    stacked = jnp.stack(group_results, axis=2)
    return stacked.reshape(ROUNDS + 1, NP * BG, BPG, PW, PW)
```

```python
import functools

import jax
import jax.numpy as jnp
from jax import lax
from jax.experimental import pallas as pl
from jax.experimental.pallas import tpu as pltpu
from jax.sharding import PartitionSpec as P

KMAX = 512
ROUNDS = 8
ALIGN = 16
LIMIT = 56 * 1024 * 1024


def project_kernel(starts, offsets, counts, snps, vectors, scores, out):
    block = pl.program_id(0)
    slab = min(out.shape[0], KMAX + ALIGN)
    start = pl.multiple_of(starts[block], ALIGN)
    low = offsets[block]
    snp_rows = lax.broadcasted_iota(jnp.int32, scores.shape[2:], 0)
    masked = jnp.where(snp_rows < snps[block], scores[0, 0].astype(jnp.float32), 0.0)
    masked = masked.astype(jnp.bfloat16)
    value = jnp.dot(vectors[pl.ds(start, slab), :], masked, preferred_element_type=jnp.float32)
    rows = start + lax.broadcasted_iota(jnp.int32, value.shape, 0)
    keep = (rows >= low) & (rows < low + counts[block])
    previous = out[pl.ds(start, slab), :].astype(jnp.float32)
    out[pl.ds(start, slab), :] = jnp.where(keep, value, previous).astype(out.dtype)


def project(vectors, scores, starts, offsets, counts, snps):
    row_total = vectors.shape[0]
    blocks, snp_rows, width = scores.shape[1:]
    return pl.pallas_call(
        project_kernel,
        out_shape=jax.ShapeDtypeStruct((row_total, width), jnp.bfloat16),
        grid_spec=pltpu.PrefetchScalarGridSpec(
            num_scalar_prefetch=4,
            grid=(blocks,),
            in_specs=[
                pl.BlockSpec(vectors.shape, lambda b, *_: (0, 0)),
                pl.BlockSpec((1, 1, snp_rows, width), lambda b, *_: (0, b, 0, 0)),
            ],
            out_specs=pl.BlockSpec((row_total, width), lambda b, *_: (0, 0)),
        ),
        compiler_params=pltpu.CompilerParams(vmem_limit_bytes=LIMIT),
    )(starts, offsets, counts, snps, vectors, scores)


def gram_kernel(starts, offsets, counts, slots, weighted, panels, scale, out):
    block = pl.program_id(0)
    slab = min(weighted.shape[0], KMAX + ALIGN)
    width = weighted.shape[1]
    start = pl.multiple_of(starts[block], ALIGN)
    low = offsets[block]
    count = counts[block]
    left = weighted[pl.ds(start, slab), :].astype(jnp.float32)
    rows = start + lax.broadcasted_iota(jnp.int32, left.shape, 0)
    keep = (rows >= low) & (rows < low + count)
    left = jnp.where(keep, left, 0.0).T.astype(jnp.bfloat16)
    for index in range(out.shape[0]):
        right = panels[slots[index], pl.ds(start, slab), :]
        gram = jnp.dot(left, right, preferred_element_type=jnp.float32)
        if index == 0:
            shape = (width, width)
            same = lax.broadcasted_iota(jnp.int32, shape, 0) == lax.broadcasted_iota(
                jnp.int32, shape, 1
            )
            gram = gram - jnp.where(same, count.astype(jnp.float32), 0.0)
        out[index, 0, 0] = gram * scale[index]


def grams(weighted, panels, scale, slots, starts, offsets, counts):
    blocks = counts.shape[0]
    rounds, width = scale.shape[:2]
    return pl.pallas_call(
        gram_kernel,
        out_shape=jax.ShapeDtypeStruct((rounds, 1, blocks, width, width), jnp.float32),
        grid_spec=pltpu.PrefetchScalarGridSpec(
            num_scalar_prefetch=4,
            grid=(blocks,),
            in_specs=[
                pl.BlockSpec(weighted.shape, lambda b, *_: (0, 0), pipeline_mode=pl.Buffered(1)),
                pl.BlockSpec(panels.shape, lambda b, *_: (0, 0, 0), pipeline_mode=pl.Buffered(1)),
                pl.BlockSpec(scale.shape, lambda b, *_: (0, 0, 0), pipeline_mode=pl.Buffered(1)),
            ],
            out_specs=pl.BlockSpec((rounds, 1, 1, width, width), lambda b, *_: (0, 0, b, 0, 0)),
        ),
        compiler_params=pltpu.CompilerParams(vmem_limit_bytes=LIMIT),
    )(starts, offsets, counts, slots, weighted, panels, scale)


def per_device(eig_vectors, eig_values, eig_count, snp_count, zscores, samples):
    devices = lax.axis_size("panel")
    spacing = max(1, devices // 32)
    panels = devices // spacing
    slot_index = lax.axis_index("panel")
    panel_index = slot_index // spacing
    group_index = slot_index % spacing
    members = [[g + spacing * i for i in range(panels)] for g in range(spacing)]
    gather = functools.partial(
        lax.all_gather, axis_name="panel", axis_index_groups=members if spacing > 1 else None
    )
    blocks_here, snp_rows, panel_width = zscores.shape[1:]
    counts = lax.dynamic_slice_in_dim(eig_count, group_index * blocks_here, blocks_here)
    snps = lax.dynamic_slice_in_dim(snp_count, group_index * blocks_here, blocks_here)
    offsets = (jnp.cumsum(counts) - counts).astype(jnp.int32)
    row_total = panels * eig_vectors.shape[0]
    slab = min(row_total, KMAX + ALIGN)
    starts = jnp.minimum(offsets // ALIGN * ALIGN, row_total - slab)
    rounds = jnp.arange(ROUNDS + 1, dtype=jnp.int32)
    partners = (panel_index - rounds) % panels
    scales = samples.astype(jnp.float32).reshape(panels, panel_width)
    own_scale = lax.dynamic_index_in_dim(scales, panel_index, 0, keepdims=False)
    scale = 1.0 / jnp.sqrt(own_scale[None, :, None] * scales[partners][:, None, :])

    vectors = gather(eig_vectors, tiled=True)
    values = gather(eig_values, tiled=True)
    projected = project(vectors, zscores, starts, offsets, counts, snps)
    held = gather(projected)
    weighted = (projected.astype(jnp.float32) / values.astype(jnp.float32)[:, None]).astype(
        jnp.bfloat16
    )
    return grams(weighted, held, scale, partners, starts, offsets, counts)


def solution(mesh):
    placed = (
        P(("groups", "panel"), None),
        P(("groups", "panel")),
        P("groups"),
        P("groups"),
        P(("groups", "panel"), None, None, None),
        P("groups"),
    )
    return jax.shard_map(
        per_device,
        mesh=mesh,
        in_specs=placed,
        out_specs=P(None, ("groups", "panel"), None, None, None),
        check_vma=False,
    )
```

```python
import functools

import jax
import jax.numpy as jnp
from jax import lax
from jax.experimental import pallas as pl
from jax.experimental.pallas import tpu as pltpu
from jax.sharding import PartitionSpec as P

ROUNDS = 8
LIMIT = 56 * 1024 * 1024


def place_masked(snps, scores, pair, store):
    width = scores.shape[-1]
    for side in range(2):
        block = 2 * pair + side
        rows = lax.broadcasted_iota(jnp.int32, scores.shape[-2:], 0)
        part = jnp.where(rows < snps[block], scores[side].astype(jnp.float32), 0.0)
        store[:, side * width : (side + 1) * width] = part.astype(jnp.bfloat16)


def project_rows(vectors, masked, first_count):
    both = jnp.dot(vectors, masked, preferred_element_type=jnp.float32)
    width = both.shape[1] // 2
    rows = lax.broadcasted_iota(jnp.int32, (both.shape[0], width), 0)
    return jnp.where(rows < first_count, both[:, :width], both[:, width:]).astype(jnp.bfloat16)


def project_kernel(counts, snps, vectors, scores, out, masked):
    pair = pl.program_id(0)
    place_masked(snps, scores.at[0], pair, masked)
    out[...] = project_rows(vectors[...], masked[...], counts[2 * pair])


def project(vectors, scores, counts, snps):
    row_total, depth = vectors.shape
    blocks, snp_rows, width = scores.shape[1:]
    pair_rows = 2 * row_total // blocks
    return pl.pallas_call(
        project_kernel,
        out_shape=jax.ShapeDtypeStruct((row_total, width), jnp.bfloat16),
        grid_spec=pltpu.PrefetchScalarGridSpec(
            num_scalar_prefetch=2,
            grid=(blocks // 2,),
            in_specs=[
                pl.BlockSpec((pair_rows, depth), lambda b, *_: (b, 0)),
                pl.BlockSpec((1, 2, snp_rows, width), lambda b, *_: (0, b, 0, 0)),
            ],
            out_specs=pl.BlockSpec((pair_rows, width), lambda b, *_: (b, 0)),
            scratch_shapes=[pltpu.VMEM((snp_rows, 2 * width), jnp.bfloat16)],
        ),
        compiler_params=pltpu.CompilerParams(vmem_limit_bytes=LIMIT),
    )(counts, snps, vectors, scores)


def gram_kernel(counts, slots, weighted, panels, scale, out):
    pair = pl.program_id(0)
    width = weighted.shape[1]
    left = weighted[...].astype(jnp.float32)
    rows = lax.broadcasted_iota(jnp.int32, left.shape, 0)
    first = rows < counts[2 * pair]
    left = jnp.concatenate([jnp.where(first, left, 0.0).T, jnp.where(first, 0.0, left).T], axis=0)
    left = left.astype(jnp.bfloat16)
    shape = (width, width)
    same = lax.broadcasted_iota(jnp.int32, shape, 0) == lax.broadcasted_iota(jnp.int32, shape, 1)
    for index in range(out.shape[0]):
        both = jnp.dot(left, panels[slots[index]], preferred_element_type=jnp.float32)
        for side in range(2):
            gram = both[side * width : (side + 1) * width]
            if index == 0:
                count = counts[2 * pair + side].astype(jnp.float32)
                gram = gram - jnp.where(same, count, 0.0)
            out[index, 0, side] = gram * scale[index]


def grams(weighted, panels, scale, slots, counts):
    blocks = counts.shape[0]
    rounds, width = scale.shape[:2]
    pair_rows = 2 * weighted.shape[0] // blocks
    return pl.pallas_call(
        gram_kernel,
        out_shape=jax.ShapeDtypeStruct((rounds, 1, blocks, width, width), jnp.float32),
        grid_spec=pltpu.PrefetchScalarGridSpec(
            num_scalar_prefetch=2,
            grid=(blocks // 2,),
            in_specs=[
                pl.BlockSpec((pair_rows, width), lambda b, *_: (b, 0)),
                pl.BlockSpec((panels.shape[0], pair_rows, width), lambda b, *_: (0, b, 0)),
                pl.BlockSpec(scale.shape, lambda b, *_: (0, 0, 0)),
            ],
            out_specs=pl.BlockSpec((rounds, 1, 2, width, width), lambda b, *_: (0, 0, b, 0, 0)),
        ),
        compiler_params=pltpu.CompilerParams(vmem_limit_bytes=LIMIT),
    )(counts, slots, weighted, panels, scale)


def exchange_kernel(counts, snps, own, own_values, scores, held, values, store, masked, here,
                    send1, recv1, send2, recv2, send3, recv3):
    line = lax.axis_size("panel") // 4
    me = lax.axis_index("panel")
    z = me // 4
    y = (me // 2) % 2
    k = me % 2
    piece = own.shape[0]
    pair_rows = 4 * piece
    halves = recv1.shape[1]
    part = piece // halves
    chunks = recv2.shape[1]
    top = line - 1
    up, down, across, beside = me + 4, me - 4, me + 2 - 4 * y, me + 1 - 2 * k
    pending = []

    barrier = pltpu.get_barrier_semaphore()
    others = 4 * line - 1
    for step in range(1, others + 1):
        target = lax.rem(me + step, others + 1)
        pl.semaphore_signal(
            barrier, inc=1, device_id={"panel": target}, device_id_type=pl.DeviceIdType.MESH
        )
    pl.semaphore_wait(barrier, others)

    def start(condition, copy):
        if condition is None:
            copy.start()
        else:
            pl.when(condition)(copy.start)
        pending.append((condition, copy))

    def move1(source, half, way, target, first=False):
        rows = pl.ds(source * piece + half * part, part)
        origin = own.at[pl.ds(half * part, part)] if first else store.at[rows]
        return pltpu.make_async_remote_copy(
            src_ref=origin,
            dst_ref=store.at[rows],
            send_sem=send1.at[way, source, half],
            recv_sem=recv1.at[source, half],
            device_id={"panel": target},
            device_id_type=pl.DeviceIdType.MESH,
        )

    def arrive1(source, half):
        move1(source, half, 0, beside).wait_recv()

    def move2(source, chunk, way, target):
        rows = pl.ds(chunk * pair_rows, pair_rows)
        return pltpu.make_async_remote_copy(
            src_ref=held.at[source, rows],
            dst_ref=held.at[source, rows],
            send_sem=send2.at[way, source, chunk],
            recv_sem=recv2.at[source, chunk],
            device_id={"panel": target},
            device_id_type=pl.DeviceIdType.MESH,
        )

    def arrive2(source, chunk):
        move2(source, chunk, 0, beside).wait_recv()

    def move3(source, step, target):
        return pltpu.make_async_remote_copy(
            src_ref=own_values,
            dst_ref=values.at[source],
            send_sem=send3.at[step],
            recv_sem=recv3.at[source],
            device_id={"panel": target},
            device_id_type=pl.DeviceIdType.MESH,
        )

    for half in range(halves):
        start(z < top, move1(me, half, 0, up, True))
        start(z > 0, move1(me, half, 1, down, True))
        start(None, move1(me, half, 2, across, True))
        start(None, move1(me, half, 3, beside, True))
    for step in range(1, others + 1):
        start(None, move3(me, step, lax.rem(me + step, others + 1)))
    local = [
        pltpu.make_async_copy(own, store.at[pl.ds(me * piece, piece)], here.at[0]),
        pltpu.make_async_copy(own_values, values.at[me], here.at[1]),
    ]
    for copy in local:
        copy.start()
    for pair in range(line):
        place_masked(snps, scores.at[0, pl.ds(2 * pair, 2)], pair, masked.at[pair])
    for copy in local:
        copy.wait()

    def plane(index):
        rows = pl.ds(index * pair_rows, pair_rows)
        held[me, rows] = project_rows(store[rows], masked[index], counts[2 * index])

    def column(distance):
        for half in range(halves):
            def below():
                arrive1(me - 4 * distance, half)
            def above():
                arrive1(me + 4 * distance, half)
            has_below, has_above = z >= distance, z + distance <= top
            pl.when(has_below)(below)
            source = me - 4 * distance
            start(has_below & (z < top), move1(source, half, 0, up))
            start(has_below, move1(source, half, 2, across))
            start(has_below, move1(source, half, 3, beside))
            pl.when(has_above)(above)
            source = me + 4 * distance
            start(has_above & (z > 0), move1(source, half, 1, down))
            start(has_above, move1(source, half, 2, across))
            start(has_above, move1(source, half, 3, beside))

    def sideways(distance, sign):
        has = (z >= distance) if sign < 0 else (z + distance <= top)
        source = across + sign * 4 * distance
        for half in range(halves):
            pl.when(has)(functools.partial(arrive1, source, half))
            start(has, move1(source, half, 3, beside))

    def finish(distance, sign):
        has = (z >= distance) if sign < 0 else (z + distance <= top)

        @pl.when(has)
        def _():
            for source in (beside, beside + 2 - 4 * y):
                for half in range(halves):
                    arrive1(source + sign * 4 * distance, half)
            plane(z + sign * distance)

    for distance in range(1, line + 1):
        if distance < line:
            column(distance)
        last = distance - 1
        signs = (1,) if last == 0 else (-1, 1)
        for sign in signs:
            sideways(last, sign)
        for sign in signs:
            finish(last, sign)

    def spread(condition, chunk, source, behind):
        side = (behind >= y) & (behind <= y + 1)
        near = behind <= 2
        start(condition & side, move2(source, chunk, 2, across))
        start(condition & near, move2(source, chunk, 3, beside))

    always = me >= 0
    cross = []
    for lag in range(2):
        plane_index = lax.rem(z - lag - (1 - y) + line, line)
        cross.append(plane_index * 4 + (1 - y) * 2 + k)
    for chunk in range(chunks):
        start(z < top, move2(me, chunk, 0, up))
        start(z >= line - 2, move2(me, chunk, 1, down))
        spread(always, chunk, me, 0)
    for chunk in range(chunks + 1):
        if chunk < chunks:
            for distance in range(1, line):
                if distance <= 2:
                    has = z >= distance
                    source = me - 4 * distance
                    pl.when(has)(functools.partial(arrive2, source, chunk))
                    if distance == 1:
                        start(has & (z < top), move2(source, chunk, 0, up))
                    spread(has, chunk, source, distance)
                has = (z + distance <= top) & (z + distance >= line - 2)
                source = me + 4 * distance
                pl.when(has)(functools.partial(arrive2, source, chunk))
                start(has & (z > 0), move2(source, chunk, 1, down))
                spread(has, chunk, source, line - distance)
        if chunk > 0:
            for source in cross:
                arrive2(source, chunk - 1)
                start(None, move2(source, chunk - 1, 3, beside))
    for chunk in range(chunks):
        for source in cross:
            arrive2(source + 1 - 2 * k, chunk)
        for behind in range(3):
            plane_index = lax.rem(z - behind + line, line)
            arrive2(plane_index * 4 + y * 2 + 1 - k, chunk)
    for step in range(1, others + 1):
        move3(lax.rem(me + step, others + 1), step, beside).wait_recv()
    for condition, copy in pending:
        if condition is None:
            copy.wait_send()
        else:
            pl.when(condition)(copy.wait_send)


def exchange(vectors, values, counts, snps, scores):
    devices = lax.axis_size("panel")
    piece, depth = vectors.shape
    blocks, snp_rows, width = scores.shape[1:]
    row_total = devices * piece
    lanes = -(-piece // 128) * 128
    rider = jnp.pad(values.astype(jnp.float32), (0, lanes - piece))
    rider = jnp.broadcast_to(rider, (8, lanes))
    halves = 2
    chunks = blocks // 2
    vmem = pl.BlockSpec(memory_space=pltpu.VMEM)
    smem = pl.BlockSpec(memory_space=pltpu.SMEM)
    held, gathered = pl.pallas_call(
        exchange_kernel,
        out_shape=(
            jax.ShapeDtypeStruct((devices, row_total, width), jnp.bfloat16),
            jax.ShapeDtypeStruct((devices, 8, lanes), jnp.float32),
        ),
        in_specs=[smem, smem, vmem, vmem, vmem],
        out_specs=(vmem, vmem),
        scratch_shapes=[
            pltpu.VMEM((row_total, depth), jnp.bfloat16),
            pltpu.VMEM((blocks // 2, snp_rows, 2 * width), jnp.bfloat16),
            pltpu.SemaphoreType.DMA((2,)),
            pltpu.SemaphoreType.DMA((4, devices, halves)),
            pltpu.SemaphoreType.DMA((devices, halves)),
            pltpu.SemaphoreType.DMA((4, devices, chunks)),
            pltpu.SemaphoreType.DMA((devices, chunks)),
            pltpu.SemaphoreType.DMA((devices,)),
            pltpu.SemaphoreType.DMA((devices,)),
        ],
        compiler_params=pltpu.CompilerParams(
            collective_id=0, has_side_effects=True, vmem_limit_bytes=LIMIT
        ),
    )(counts, snps, vectors, rider, scores)
    return held, gathered[:, 0, :piece].reshape(-1)


def per_device(eig_vectors, eig_values, eig_count, snp_count, zscores, samples):
    devices = lax.axis_size("panel")
    spacing = max(1, devices // 32)
    panels = devices // spacing
    slot_index = lax.axis_index("panel")
    panel_index = slot_index // spacing
    group_index = slot_index % spacing
    blocks_here, snp_rows, panel_width = zscores.shape[1:]
    counts = lax.dynamic_slice_in_dim(eig_count, group_index * blocks_here, blocks_here)
    snps = lax.dynamic_slice_in_dim(snp_count, group_index * blocks_here, blocks_here)
    rounds = jnp.arange(ROUNDS + 1, dtype=jnp.int32)
    partners = (panel_index - rounds) % panels
    scales = samples.astype(jnp.float32).reshape(panels, panel_width)
    own_scale = lax.dynamic_index_in_dim(scales, panel_index, 0, keepdims=False)
    scale = 1.0 / jnp.sqrt(own_scale[None, :, None] * scales[partners][:, None, :])

    if spacing == 1 and panels == 2 * ROUNDS and blocks_here == panels // 2:
        held, values = exchange(eig_vectors, eig_values, counts, snps, zscores)
        projected = lax.dynamic_index_in_dim(held, panel_index, 0, keepdims=False)
    else:
        members = [[g + spacing * i for i in range(panels)] for g in range(spacing)]
        gather = functools.partial(
            lax.all_gather, axis_name="panel", axis_index_groups=members if spacing > 1 else None
        )
        vectors = gather(eig_vectors, tiled=True)
        values = gather(eig_values, tiled=True)
        projected = project(vectors, zscores, counts, snps)
        held = gather(projected)
    weighted = (projected.astype(jnp.float32) / values.astype(jnp.float32)[:, None]).astype(
        jnp.bfloat16
    )
    return grams(weighted, held, scale, partners, counts)


def solution(mesh):
    placed = (
        P(("groups", "panel"), None),
        P(("groups", "panel")),
        P("groups"),
        P("groups"),
        P(("groups", "panel"), None, None, None),
        P("groups"),
    )
    return jax.shard_map(
        per_device,
        mesh=mesh,
        in_specs=placed,
        out_specs=P(None, ("groups", "panel"), None, None, None),
        check_vma=False,
    )
```

```python
import functools

import jax
import jax.numpy as jnp
from jax import lax
from jax.experimental import pallas as pl
from jax.experimental.pallas import tpu as pltpu
from jax.sharding import PartitionSpec as P

ROUNDS = 8
LIMIT = 56 * 1024 * 1024


def place_masked(snps, scores, pair, store):
    width = scores.shape[-1]
    for side in range(2):
        block = 2 * pair + side
        rows = lax.broadcasted_iota(jnp.int32, scores.shape[-2:], 0)
        part = jnp.where(rows < snps[block], scores[side].astype(jnp.float32), 0.0)
        store[:, side * width : (side + 1) * width] = part.astype(jnp.bfloat16)


def project_rows(vectors, masked, first_count):
    both = jnp.dot(vectors, masked, preferred_element_type=jnp.float32)
    width = both.shape[1] // 2
    rows = lax.broadcasted_iota(jnp.int32, (both.shape[0], width), 0)
    return jnp.where(rows < first_count, both[:, :width], both[:, width:]).astype(jnp.bfloat16)


def project_kernel(counts, snps, vectors, scores, out, masked):
    pair = pl.program_id(0)
    place_masked(snps, scores.at[0], pair, masked)
    out[...] = project_rows(vectors[...], masked[...], counts[2 * pair])


def project(vectors, scores, counts, snps):
    row_total, depth = vectors.shape
    blocks, snp_rows, width = scores.shape[1:]
    pair_rows = 2 * row_total // blocks
    return pl.pallas_call(
        project_kernel,
        out_shape=jax.ShapeDtypeStruct((row_total, width), jnp.bfloat16),
        grid_spec=pltpu.PrefetchScalarGridSpec(
            num_scalar_prefetch=2,
            grid=(blocks // 2,),
            in_specs=[
                pl.BlockSpec((pair_rows, depth), lambda b, *_: (b, 0)),
                pl.BlockSpec((1, 2, snp_rows, width), lambda b, *_: (0, b, 0, 0)),
            ],
            out_specs=pl.BlockSpec((pair_rows, width), lambda b, *_: (b, 0)),
            scratch_shapes=[pltpu.VMEM((snp_rows, 2 * width), jnp.bfloat16)],
        ),
        compiler_params=pltpu.CompilerParams(vmem_limit_bytes=LIMIT),
    )(counts, snps, vectors, scores)


def gram_kernel(counts, slots, weighted, panels, scale, out):
    pair = pl.program_id(0)
    width = weighted.shape[1]
    left = weighted[...].astype(jnp.float32)
    rows = lax.broadcasted_iota(jnp.int32, left.shape, 0)
    first = rows < counts[2 * pair]
    left = jnp.concatenate([jnp.where(first, left, 0.0).T, jnp.where(first, 0.0, left).T], axis=0)
    left = left.astype(jnp.bfloat16)
    shape = (width, width)
    same = lax.broadcasted_iota(jnp.int32, shape, 0) == lax.broadcasted_iota(jnp.int32, shape, 1)
    for index in range(out.shape[0]):
        both = jnp.dot(left, panels[slots[index]], preferred_element_type=jnp.float32)
        for side in range(2):
            gram = both[side * width : (side + 1) * width]
            if index == 0:
                count = counts[2 * pair + side].astype(jnp.float32)
                gram = gram - jnp.where(same, count, 0.0)
            out[index, 0, side] = gram * scale[index]


def grams(weighted, panels, scale, slots, counts):
    blocks = counts.shape[0]
    rounds, width = scale.shape[:2]
    pair_rows = 2 * weighted.shape[0] // blocks
    return pl.pallas_call(
        gram_kernel,
        out_shape=jax.ShapeDtypeStruct((rounds, 1, blocks, width, width), jnp.float32),
        grid_spec=pltpu.PrefetchScalarGridSpec(
            num_scalar_prefetch=2,
            grid=(blocks // 2,),
            in_specs=[
                pl.BlockSpec((pair_rows, width), lambda b, *_: (b, 0)),
                pl.BlockSpec((panels.shape[0], pair_rows, width), lambda b, *_: (0, b, 0)),
                pl.BlockSpec(scale.shape, lambda b, *_: (0, 0, 0)),
            ],
            out_specs=pl.BlockSpec((rounds, 1, 2, width, width), lambda b, *_: (0, 0, b, 0, 0)),
        ),
        compiler_params=pltpu.CompilerParams(vmem_limit_bytes=LIMIT),
    )(counts, slots, weighted, panels, scale)


def exchange_kernel(counts, snps, own, own_values, scores, held, values, store, masked, here,
                    send1, recv1, send2, recv2, send3, recv3):
    line = lax.axis_size("panel") // 4
    me = lax.axis_index("panel")
    z = me // 4
    y = (me // 2) % 2
    k = me % 2
    piece = own.shape[0]
    pair_rows = 4 * piece
    halves = recv1.shape[1]
    part = piece // halves
    chunks = recv2.shape[1]
    top = line - 1
    up, down, across, beside = me + 4, me - 4, me + 2 - 4 * y, me + 1 - 2 * k
    pending = []

    barrier = pltpu.get_barrier_semaphore()
    others = 4 * line - 1
    for step in range(1, others + 1):
        target = lax.rem(me + step, others + 1)
        pl.semaphore_signal(
            barrier, inc=1, device_id={"panel": target}, device_id_type=pl.DeviceIdType.MESH
        )
    pl.semaphore_wait(barrier, others)

    def start(condition, copy):
        if condition is None:
            copy.start()
        else:
            pl.when(condition)(copy.start)
        pending.append((condition, copy))

    def move1(source, half, way, target, first=False):
        rows = pl.ds(source * piece + half * part, part)
        origin = own.at[pl.ds(half * part, part)] if first else store.at[rows]
        return pltpu.make_async_remote_copy(
            src_ref=origin,
            dst_ref=store.at[rows],
            send_sem=send1.at[way, source, half],
            recv_sem=recv1.at[source, half],
            device_id={"panel": target},
            device_id_type=pl.DeviceIdType.MESH,
        )

    def arrive1(source, half):
        move1(source, half, 0, beside).wait_recv()

    def move2(source, chunk, way, target):
        rows = pl.ds(chunk * pair_rows, pair_rows)
        return pltpu.make_async_remote_copy(
            src_ref=held.at[source, rows],
            dst_ref=held.at[source, rows],
            send_sem=send2.at[way, source, chunk],
            recv_sem=recv2.at[source, chunk],
            device_id={"panel": target},
            device_id_type=pl.DeviceIdType.MESH,
        )

    def arrive2(source, chunk):
        move2(source, chunk, 0, beside).wait_recv()

    def move3(source, step, target):
        return pltpu.make_async_remote_copy(
            src_ref=own_values,
            dst_ref=values.at[source],
            send_sem=send3.at[step],
            recv_sem=recv3.at[source],
            device_id={"panel": target},
            device_id_type=pl.DeviceIdType.MESH,
        )

    def spread(condition, chunk, source, behind):
        side = (behind >= y) & (behind <= y + 1)
        near = behind <= 2
        start(condition & side, move2(source, chunk, 2, across))
        start(condition & near, move2(source, chunk, 3, beside))

    def order(source, step):
        far = source // 4
        near = jnp.minimum(far, top - far)
        nearest = jnp.where(step > 2 * near, step, (near + (step + 1) // 2 * (1 - 2 * (step % 2))))
        return jnp.where(far > top - far, top - nearest, nearest)

    for half in range(halves):
        start(z < top, move1(me, half, 0, up, True))
        start(z > 0, move1(me, half, 1, down, True))
        start(None, move1(me, half, 2, across, True))
        start(None, move1(me, half, 3, beside, True))
    for step in range(1, others + 1):
        start(None, move3(me, step, lax.rem(me + step, others + 1)))
    local = [
        pltpu.make_async_copy(own, store.at[pl.ds(me * piece, piece)], here.at[0]),
        pltpu.make_async_copy(own_values, values.at[me], here.at[1]),
    ]
    for copy in local:
        copy.start()
    for pair in range(line):
        place_masked(snps, scores.at[0, pl.ds(2 * pair, 2)], pair, masked.at[pair])
    for copy in local:
        copy.wait()

    def plane(index):
        rows = pl.ds(index * pair_rows, pair_rows)
        held[me, rows] = project_rows(store[rows], masked[index], counts[2 * index])

    def column(distance):
        for half in range(halves):
            def below():
                arrive1(me - 4 * distance, half)
            def above():
                arrive1(me + 4 * distance, half)
            has_below, has_above = z >= distance, z + distance <= top
            pl.when(has_below)(below)
            source = me - 4 * distance
            start(has_below & (z < top), move1(source, half, 0, up))
            start(has_below, move1(source, half, 2, across))
            start(has_below, move1(source, half, 3, beside))
            pl.when(has_above)(above)
            source = me + 4 * distance
            start(has_above & (z > 0), move1(source, half, 1, down))
            start(has_above, move1(source, half, 2, across))
            start(has_above, move1(source, half, 3, beside))

    def sideways(distance, sign):
        has = (z >= distance) if sign < 0 else (z + distance <= top)
        source = across + sign * 4 * distance
        for half in range(halves):
            pl.when(has)(functools.partial(arrive1, source, half))
            start(has, move1(source, half, 3, beside))

    def finish(distance, sign):
        has = (z >= distance) if sign < 0 else (z + distance <= top)

        @pl.when(has)
        def _():
            for source in (beside, beside + 2 - 4 * y):
                for half in range(halves):
                    arrive1(source + sign * 4 * distance, half)
            plane(z + sign * distance)

        chunk = z + sign * distance
        start(has & (z < top), move2(me, chunk, 0, up))
        start(has & (z >= line - 2), move2(me, chunk, 1, down))
        spread(has, chunk, me, 0)

    for distance in range(1, line + 1):
        if distance < line:
            column(distance)
        last = distance - 1
        signs = (1,) if last == 0 else (-1, 1)
        for sign in signs:
            sideways(last, sign)
        for sign in signs:
            finish(last, sign)

    cross = []
    for lag in range(2):
        plane_index = lax.rem(z - lag - (1 - y) + line, line)
        cross.append(plane_index * 4 + (1 - y) * 2 + k)
    for step in range(chunks + 1):
        if step < chunks:
            for distance in range(1, line):
                if distance <= 2:
                    has = z >= distance
                    source = me - 4 * distance
                    chunk = order(source, step)
                    pl.when(has)(functools.partial(arrive2, source, chunk))
                    if distance == 1:
                        start(has & (z < top), move2(source, chunk, 0, up))
                    spread(has, chunk, source, distance)
                has = (z + distance <= top) & (z + distance >= line - 2)
                source = me + 4 * distance
                chunk = order(source, step)
                pl.when(has)(functools.partial(arrive2, source, chunk))
                start(has & (z > 0), move2(source, chunk, 1, down))
                spread(has, chunk, source, line - distance)
        if step > 0:
            for source in cross:
                chunk = order(source, step - 1)
                arrive2(source, chunk)
                start(None, move2(source, chunk, 3, beside))
    for chunk in range(chunks):
        for source in cross:
            arrive2(source + 1 - 2 * k, chunk)
        for behind in range(3):
            plane_index = lax.rem(z - behind + line, line)
            arrive2(plane_index * 4 + y * 2 + 1 - k, chunk)
    for step in range(1, others + 1):
        move3(lax.rem(me + step, others + 1), step, beside).wait_recv()
    for condition, copy in pending:
        if condition is None:
            copy.wait_send()
        else:
            pl.when(condition)(copy.wait_send)


def exchange(vectors, values, counts, snps, scores):
    devices = lax.axis_size("panel")
    piece, depth = vectors.shape
    blocks, snp_rows, width = scores.shape[1:]
    row_total = devices * piece
    lanes = -(-piece // 128) * 128
    rider = jnp.pad(values.astype(jnp.float32), (0, lanes - piece))
    rider = jnp.broadcast_to(rider, (8, lanes))
    halves = 2
    chunks = blocks // 2
    vmem = pl.BlockSpec(memory_space=pltpu.VMEM)
    smem = pl.BlockSpec(memory_space=pltpu.SMEM)
    held, gathered = pl.pallas_call(
        exchange_kernel,
        out_shape=(
            jax.ShapeDtypeStruct((devices, row_total, width), jnp.bfloat16),
            jax.ShapeDtypeStruct((devices, 8, lanes), jnp.float32),
        ),
        in_specs=[smem, smem, vmem, vmem, vmem],
        out_specs=(vmem, vmem),
        scratch_shapes=[
            pltpu.VMEM((row_total, depth), jnp.bfloat16),
            pltpu.VMEM((blocks // 2, snp_rows, 2 * width), jnp.bfloat16),
            pltpu.SemaphoreType.DMA((2,)),
            pltpu.SemaphoreType.DMA((4, devices, halves)),
            pltpu.SemaphoreType.DMA((devices, halves)),
            pltpu.SemaphoreType.DMA((4, devices, chunks)),
            pltpu.SemaphoreType.DMA((devices, chunks)),
            pltpu.SemaphoreType.DMA((devices,)),
            pltpu.SemaphoreType.DMA((devices,)),
        ],
        compiler_params=pltpu.CompilerParams(
            collective_id=0, has_side_effects=True, vmem_limit_bytes=LIMIT
        ),
    )(counts, snps, vectors, rider, scores)
    return held, gathered[:, 0, :piece].reshape(-1)


def per_device(eig_vectors, eig_values, eig_count, snp_count, zscores, samples):
    devices = lax.axis_size("panel")
    spacing = max(1, devices // 32)
    panels = devices // spacing
    slot_index = lax.axis_index("panel")
    panel_index = slot_index // spacing
    group_index = slot_index % spacing
    blocks_here, snp_rows, panel_width = zscores.shape[1:]
    counts = lax.dynamic_slice_in_dim(eig_count, group_index * blocks_here, blocks_here)
    snps = lax.dynamic_slice_in_dim(snp_count, group_index * blocks_here, blocks_here)
    rounds = jnp.arange(ROUNDS + 1, dtype=jnp.int32)
    partners = (panel_index - rounds) % panels
    scales = samples.astype(jnp.float32).reshape(panels, panel_width)
    own_scale = lax.dynamic_index_in_dim(scales, panel_index, 0, keepdims=False)
    scale = 1.0 / jnp.sqrt(own_scale[None, :, None] * scales[partners][:, None, :])

    if spacing == 1 and panels == 2 * ROUNDS and blocks_here == panels // 2:
        held, values = exchange(eig_vectors, eig_values, counts, snps, zscores)
        projected = lax.dynamic_index_in_dim(held, panel_index, 0, keepdims=False)
    else:
        members = [[g + spacing * i for i in range(panels)] for g in range(spacing)]
        gather = functools.partial(
            lax.all_gather, axis_name="panel", axis_index_groups=members if spacing > 1 else None
        )
        vectors = gather(eig_vectors, tiled=True)
        values = gather(eig_values, tiled=True)
        projected = project(vectors, zscores, counts, snps)
        held = gather(projected)
    weighted = (projected.astype(jnp.float32) / values.astype(jnp.float32)[:, None]).astype(
        jnp.bfloat16
    )
    return grams(weighted, held, scale, partners, counts)


def solution(mesh):
    placed = (
        P(("groups", "panel"), None),
        P(("groups", "panel")),
        P("groups"),
        P("groups"),
        P(("groups", "panel"), None, None, None),
        P("groups"),
    )
    return jax.shard_map(
        per_device,
        mesh=mesh,
        in_specs=placed,
        out_specs=P(None, ("groups", "panel"), None, None, None),
        check_vma=False,
    )
```

```python
import functools

import jax
import jax.numpy as jnp
from jax import lax
from jax.experimental import pallas as pl
from jax.experimental.pallas import tpu as pltpu
from jax.sharding import PartitionSpec as P

ROUNDS = 8
LIMIT = 56 * 1024 * 1024


def place_masked(snps, scores, pair, store):
    width = scores.shape[-1]
    for side in range(2):
        block = 2 * pair + side
        rows = lax.broadcasted_iota(jnp.int32, scores.shape[-2:], 0)
        part = jnp.where(rows < snps[block], scores[side].astype(jnp.float32), 0.0)
        store[:, side * width : (side + 1) * width] = part.astype(jnp.bfloat16)


def project_rows(vectors, masked, first_count):
    both = jnp.dot(vectors, masked, preferred_element_type=jnp.float32)
    width = both.shape[1] // 2
    rows = lax.broadcasted_iota(jnp.int32, (both.shape[0], width), 0)
    return jnp.where(rows < first_count, both[:, :width], both[:, width:]).astype(jnp.bfloat16)


def project_kernel(counts, snps, vectors, scores, out, masked):
    pair = pl.program_id(0)
    place_masked(snps, scores.at[0], pair, masked)
    out[...] = project_rows(vectors[...], masked[...], counts[2 * pair])


def project(vectors, scores, counts, snps):
    row_total, depth = vectors.shape
    blocks, snp_rows, width = scores.shape[1:]
    pair_rows = 2 * row_total // blocks
    return pl.pallas_call(
        project_kernel,
        out_shape=jax.ShapeDtypeStruct((row_total, width), jnp.bfloat16),
        grid_spec=pltpu.PrefetchScalarGridSpec(
            num_scalar_prefetch=2,
            grid=(blocks // 2,),
            in_specs=[
                pl.BlockSpec((pair_rows, depth), lambda b, *_: (b, 0)),
                pl.BlockSpec((1, 2, snp_rows, width), lambda b, *_: (0, b, 0, 0)),
            ],
            out_specs=pl.BlockSpec((pair_rows, width), lambda b, *_: (b, 0)),
            scratch_shapes=[pltpu.VMEM((snp_rows, 2 * width), jnp.bfloat16)],
        ),
        compiler_params=pltpu.CompilerParams(vmem_limit_bytes=LIMIT),
    )(counts, snps, vectors, scores)


def gram_kernel(counts, slots, weighted, panels, scale, out):
    pair = pl.program_id(0)
    width = weighted.shape[1]
    left = weighted[...].astype(jnp.float32)
    rows = lax.broadcasted_iota(jnp.int32, left.shape, 0)
    first = rows < counts[2 * pair]
    left = jnp.concatenate([jnp.where(first, left, 0.0).T, jnp.where(first, 0.0, left).T], axis=0)
    left = left.astype(jnp.bfloat16)
    shape = (width, width)
    same = lax.broadcasted_iota(jnp.int32, shape, 0) == lax.broadcasted_iota(jnp.int32, shape, 1)
    for index in range(out.shape[0]):
        both = jnp.dot(left, panels[slots[index]], preferred_element_type=jnp.float32)
        for side in range(2):
            gram = both[side * width : (side + 1) * width]
            if index == 0:
                count = counts[2 * pair + side].astype(jnp.float32)
                gram = gram - jnp.where(same, count, 0.0)
            out[index, 0, side] = gram * scale[index]


def grams(weighted, panels, scale, slots, counts):
    blocks = counts.shape[0]
    rounds, width = scale.shape[:2]
    pair_rows = 2 * weighted.shape[0] // blocks
    return pl.pallas_call(
        gram_kernel,
        out_shape=jax.ShapeDtypeStruct((rounds, 1, blocks, width, width), jnp.float32),
        grid_spec=pltpu.PrefetchScalarGridSpec(
            num_scalar_prefetch=2,
            grid=(blocks // 2,),
            in_specs=[
                pl.BlockSpec((pair_rows, width), lambda b, *_: (b, 0)),
                pl.BlockSpec((panels.shape[0], pair_rows, width), lambda b, *_: (0, b, 0)),
                pl.BlockSpec(scale.shape, lambda b, *_: (0, 0, 0)),
            ],
            out_specs=pl.BlockSpec((rounds, 1, 2, width, width), lambda b, *_: (0, 0, b, 0, 0)),
        ),
        compiler_params=pltpu.CompilerParams(vmem_limit_bytes=LIMIT),
    )(counts, slots, weighted, panels, scale)


def exchange_kernel(counts, snps, own, own_values, scores, out, held, values, left, store, masked,
                    here, send1, recv1, send2, recv2, send3, recv3):
    line = lax.axis_size("panel") // 4
    me = lax.axis_index("panel")
    z = me // 4
    y = (me // 2) % 2
    k = me % 2
    piece = own.shape[0]
    pair_rows = 4 * piece
    halves = recv1.shape[1]
    part = piece // halves
    chunks = recv2.shape[1]
    top = line - 1
    up, down, across, beside = me + 4, me - 4, me + 2 - 4 * y, me + 1 - 2 * k
    pending = []

    barrier = pltpu.get_barrier_semaphore()
    others = 4 * line - 1
    for step in range(1, others + 1):
        target = lax.rem(me + step, others + 1)
        pl.semaphore_signal(
            barrier, inc=1, device_id={"panel": target}, device_id_type=pl.DeviceIdType.MESH
        )
    pl.semaphore_wait(barrier, others)

    def start(condition, copy):
        if condition is None:
            copy.start()
        else:
            pl.when(condition)(copy.start)
        pending.append((condition, copy))

    def move1(source, half, way, target, first=False):
        rows = pl.ds(source * piece + half * part, part)
        origin = own.at[pl.ds(half * part, part)] if first else store.at[rows]
        return pltpu.make_async_remote_copy(
            src_ref=origin,
            dst_ref=store.at[rows],
            send_sem=send1.at[way, source, half],
            recv_sem=recv1.at[source, half],
            device_id={"panel": target},
            device_id_type=pl.DeviceIdType.MESH,
        )

    def arrive1(source, half):
        move1(source, half, 0, beside).wait_recv()

    def move2(source, chunk, way, target):
        rows = pl.ds(chunk * pair_rows, pair_rows)
        return pltpu.make_async_remote_copy(
            src_ref=held.at[source, rows],
            dst_ref=held.at[source, rows],
            send_sem=send2.at[way, source, chunk],
            recv_sem=recv2.at[source, chunk],
            device_id={"panel": target},
            device_id_type=pl.DeviceIdType.MESH,
        )

    def arrive2(source, chunk):
        move2(source, chunk, 0, beside).wait_recv()

    def move3(source, step, target):
        return pltpu.make_async_remote_copy(
            src_ref=own_values,
            dst_ref=values.at[source],
            send_sem=send3.at[step],
            recv_sem=recv3.at[source],
            device_id={"panel": target},
            device_id_type=pl.DeviceIdType.MESH,
        )

    def spread(condition, chunk, source, behind):
        side = (behind >= y) & (behind <= y + 1)
        near = behind <= 2
        start(condition & side, move2(source, chunk, 2, across))
        start(condition & near, move2(source, chunk, 3, beside))

    def order(source, step):
        far = source // 4
        near = jnp.minimum(far, top - far)
        nearest = jnp.where(step > 2 * near, step, (near + (step + 1) // 2 * (1 - 2 * (step % 2))))
        return jnp.where(far > top - far, top - nearest, nearest)

    for half in range(halves):
        start(z < top, move1(me, half, 0, up, True))
        start(z > 0, move1(me, half, 1, down, True))
        start(None, move1(me, half, 2, across, True))
        start(None, move1(me, half, 3, beside, True))
    for step in range(1, others + 1):
        start(None, move3(me, step, lax.rem(me + step, others + 1)))
    local = [
        pltpu.make_async_copy(own, store.at[pl.ds(me * piece, piece)], here.at[0]),
        pltpu.make_async_copy(own_values, values.at[me], here.at[1]),
    ]
    for copy in local:
        copy.start()
    for pair in range(line):
        place_masked(snps, scores.at[0, pl.ds(2 * pair, 2)], pair, masked.at[pair])
    for copy in local:
        copy.wait()

    def plane(index):
        rows = pl.ds(index * pair_rows, pair_rows)
        held[me, rows] = project_rows(store[rows], masked[index], counts[2 * index])

    def column(distance):
        for half in range(halves):
            def below():
                arrive1(me - 4 * distance, half)
            def above():
                arrive1(me + 4 * distance, half)
            has_below, has_above = z >= distance, z + distance <= top
            pl.when(has_below)(below)
            source = me - 4 * distance
            start(has_below & (z < top), move1(source, half, 0, up))
            start(has_below, move1(source, half, 2, across))
            start(has_below, move1(source, half, 3, beside))
            pl.when(has_above)(above)
            source = me + 4 * distance
            start(has_above & (z > 0), move1(source, half, 1, down))
            start(has_above, move1(source, half, 2, across))
            start(has_above, move1(source, half, 3, beside))

    def sideways(distance, sign):
        has = (z >= distance) if sign < 0 else (z + distance <= top)
        source = across + sign * 4 * distance
        for half in range(halves):
            pl.when(has)(functools.partial(arrive1, source, half))
            start(has, move1(source, half, 3, beside))

    def finish(distance, sign):
        has = (z >= distance) if sign < 0 else (z + distance <= top)

        @pl.when(has)
        def _():
            for source in (beside, beside + 2 - 4 * y):
                for half in range(halves):
                    arrive1(source + sign * 4 * distance, half)
            plane(z + sign * distance)

        chunk = z + sign * distance
        start(has & (z < top), move2(me, chunk, 0, up))
        start(has & (z >= line - 2), move2(me, chunk, 1, down))
        spread(has, chunk, me, 0)

    for distance in range(1, line + 1):
        if distance < line:
            column(distance)
        last = distance - 1
        signs = (1,) if last == 0 else (-1, 1)
        for sign in signs:
            sideways(last, sign)
        for sign in signs:
            finish(last, sign)

    cross = []
    for lag in range(2):
        plane_index = lax.rem(z - lag - (1 - y) + line, line)
        cross.append(plane_index * 4 + (1 - y) * 2 + k)
    def weigh(index):
        rows = pl.ds(index * pair_rows, pair_rows)
        row = values[4 * index] + values[4 * index + 1]
        row = row + (values[4 * index + 2] + values[4 * index + 3])
        flat = held[me, rows].astype(jnp.float32).T / row[0:1]
        first = lax.broadcasted_iota(jnp.int32, flat.shape, 1) < counts[2 * index]
        both = jnp.concatenate([jnp.where(first, flat, 0.0), jnp.where(first, 0.0, flat)], axis=0)
        left[index] = both.astype(jnp.bfloat16)

    def gram(source, chunk, number, own_panel=False):
        rows = pl.ds(chunk * pair_rows, pair_rows)
        both = jnp.dot(left[chunk], held[source, rows], preferred_element_type=jnp.float32)
        width = both.shape[1]
        for side in range(2):
            part = both[side * width : (side + 1) * width]
            if own_panel:
                shape = (width, width)
                across_rows = lax.broadcasted_iota(jnp.int32, shape, 0)
                same = across_rows == lax.broadcasted_iota(jnp.int32, shape, 1)
                count = counts[2 * chunk + side].astype(jnp.float32)
                part = part - jnp.where(same, count, 0.0)
            out[number, 0, 2 * chunk + side] = part

    near = [lax.rem(z - lag + line, line) * 4 + y * 2 + k for lag in range(3)]
    swap = 1 - 2 * k

    for step in range(chunks + 2):
        if step < chunks:
            for distance in range(1, line):
                if distance <= 2:
                    has = z >= distance
                    source = me - 4 * distance
                    chunk = order(source, step)
                    pl.when(has)(functools.partial(arrive2, source, chunk))
                    if distance == 1:
                        start(has & (z < top), move2(source, chunk, 0, up))
                    spread(has, chunk, source, distance)
                has = (z + distance <= top) & (z + distance >= line - 2)
                source = me + 4 * distance
                chunk = order(source, step)
                pl.when(has)(functools.partial(arrive2, source, chunk))
                start(has & (z > 0), move2(source, chunk, 1, down))
                spread(has, chunk, source, line - distance)
        if step == 0:
            for number in range(1, others + 1):
                move3(lax.rem(me + number, others + 1), number, beside).wait_recv()
            for index in range(chunks):
                weigh(index)
        if 0 < step <= chunks:
            for source in cross:
                chunk = order(source, step - 1)
                arrive2(source, chunk)
                start(None, move2(source, chunk, 3, beside))
        if 0 < step <= chunks:
            for lag, source in enumerate(near):
                gram(source, order(source, step - 1), 4 * lag, lag == 0)
            for lag, source in enumerate(cross):
                gram(source, order(source, step - 1), 4 * lag + 2)
        if step > 1:
            for lag, source in enumerate(near):
                chunk = order(source, step - 2)
                arrive2(source + swap, chunk)
                number = 4 * lag - swap

                @pl.when((number >= 0) & (number < out.shape[0]))
                def _():
                    gram(source + swap, chunk, number)

            for lag, source in enumerate(cross):
                chunk = order(source, step - 2)
                arrive2(source + swap, chunk)
                gram(source + swap, chunk, 4 * lag + 2 - swap)
    for condition, copy in pending:
        if condition is None:
            copy.wait_send()
        else:
            pl.when(condition)(copy.wait_send)


def exchange(vectors, values, counts, snps, scores):
    devices = lax.axis_size("panel")
    piece, depth = vectors.shape
    blocks, snp_rows, width = scores.shape[1:]
    row_total = devices * piece
    pair_rows = 4 * piece
    place = lax.rem(lax.axis_index("panel"), 4) * piece
    rider = jnp.zeros((8, pair_rows), jnp.float32)
    spread = jnp.broadcast_to(values.astype(jnp.float32), (8, piece))
    rider = lax.dynamic_update_slice_in_dim(rider, spread, place, 1)
    halves = 2
    chunks = blocks // 2
    vmem = pl.BlockSpec(memory_space=pltpu.VMEM)
    smem = pl.BlockSpec(memory_space=pltpu.SMEM)
    return pl.pallas_call(
        exchange_kernel,
        out_shape=jax.ShapeDtypeStruct((ROUNDS + 1, 1, blocks, width, width), jnp.float32),
        in_specs=[smem, smem, vmem, vmem, vmem],
        out_specs=vmem,
        scratch_shapes=[
            pltpu.VMEM((devices, row_total, width), jnp.bfloat16),
            pltpu.VMEM((devices, 8, pair_rows), jnp.float32),
            pltpu.VMEM((chunks, 2 * width, pair_rows), jnp.bfloat16),
            pltpu.VMEM((row_total, depth), jnp.bfloat16),
            pltpu.VMEM((blocks // 2, snp_rows, 2 * width), jnp.bfloat16),
            pltpu.SemaphoreType.DMA((2,)),
            pltpu.SemaphoreType.DMA((4, devices, halves)),
            pltpu.SemaphoreType.DMA((devices, halves)),
            pltpu.SemaphoreType.DMA((4, devices, chunks)),
            pltpu.SemaphoreType.DMA((devices, chunks)),
            pltpu.SemaphoreType.DMA((devices,)),
            pltpu.SemaphoreType.DMA((devices,)),
        ],
        compiler_params=pltpu.CompilerParams(
            collective_id=0, has_side_effects=True, vmem_limit_bytes=LIMIT
        ),
    )(counts, snps, vectors, rider, scores)


def per_device(eig_vectors, eig_values, eig_count, snp_count, zscores, samples):
    devices = lax.axis_size("panel")
    spacing = max(1, devices // 32)
    panels = devices // spacing
    slot_index = lax.axis_index("panel")
    panel_index = slot_index // spacing
    group_index = slot_index % spacing
    blocks_here, snp_rows, panel_width = zscores.shape[1:]
    counts = lax.dynamic_slice_in_dim(eig_count, group_index * blocks_here, blocks_here)
    snps = lax.dynamic_slice_in_dim(snp_count, group_index * blocks_here, blocks_here)
    rounds = jnp.arange(ROUNDS + 1, dtype=jnp.int32)
    partners = (panel_index - rounds) % panels
    scales = samples.astype(jnp.float32).reshape(panels, panel_width)
    own_scale = lax.dynamic_index_in_dim(scales, panel_index, 0, keepdims=False)
    scale = 1.0 / jnp.sqrt(own_scale[None, :, None] * scales[partners][:, None, :])

    if spacing == 1 and panels == 2 * ROUNDS and blocks_here == panels // 2:
        raw = exchange(eig_vectors, eig_values, counts, snps, zscores)
        return raw * scale[:, None, None]
    members = [[g + spacing * i for i in range(panels)] for g in range(spacing)]
    gather = functools.partial(
        lax.all_gather, axis_name="panel", axis_index_groups=members if spacing > 1 else None
    )
    vectors = gather(eig_vectors, tiled=True)
    values = gather(eig_values, tiled=True)
    projected = project(vectors, zscores, counts, snps)
    held = gather(projected)
    weighted = (projected.astype(jnp.float32) / values.astype(jnp.float32)[:, None]).astype(
        jnp.bfloat16
    )
    return grams(weighted, held, scale, partners, counts)


def solution(mesh):
    placed = (
        P(("groups", "panel"), None),
        P(("groups", "panel")),
        P("groups"),
        P("groups"),
        P(("groups", "panel"), None, None, None),
        P("groups"),
    )
    return jax.shard_map(
        per_device,
        mesh=mesh,
        in_specs=placed,
        out_specs=P(None, ("groups", "panel"), None, None, None),
        check_vma=False,
    )
```

```python
import functools

import jax
import jax.numpy as jnp
from jax import lax
from jax.experimental import pallas as pl
from jax.experimental.pallas import tpu as pltpu
from jax.sharding import PartitionSpec as P

ROUNDS = 8
HALVES = 5
CUTS = 2
LIMIT = 56 * 1024 * 1024


def place_masked(snps, scores, pair, store):
    width = scores.shape[-1]
    for side in range(2):
        block = 2 * pair + side
        rows = lax.broadcasted_iota(jnp.int32, scores.shape[-2:], 0)
        part = jnp.where(rows < snps[block], scores[side].astype(jnp.float32), 0.0)
        store[:, side * width : (side + 1) * width] = part.astype(jnp.bfloat16)


def project_rows(vectors, masked, first_count):
    both = jnp.dot(vectors, masked, preferred_element_type=jnp.float32)
    width = both.shape[1] // 2
    rows = lax.broadcasted_iota(jnp.int32, (both.shape[0], width), 0)
    return jnp.where(rows < first_count, both[:, :width], both[:, width:]).astype(jnp.bfloat16)


def project_kernel(counts, snps, vectors, scores, out, masked):
    pair = pl.program_id(0)
    place_masked(snps, scores.at[0], pair, masked)
    out[...] = project_rows(vectors[...], masked[...], counts[2 * pair])


def project(vectors, scores, counts, snps):
    row_total, depth = vectors.shape
    blocks, snp_rows, width = scores.shape[1:]
    pair_rows = 2 * row_total // blocks
    return pl.pallas_call(
        project_kernel,
        out_shape=jax.ShapeDtypeStruct((row_total, width), jnp.bfloat16),
        grid_spec=pltpu.PrefetchScalarGridSpec(
            num_scalar_prefetch=2,
            grid=(blocks // 2,),
            in_specs=[
                pl.BlockSpec((pair_rows, depth), lambda b, *_: (b, 0)),
                pl.BlockSpec((1, 2, snp_rows, width), lambda b, *_: (0, b, 0, 0)),
            ],
            out_specs=pl.BlockSpec((pair_rows, width), lambda b, *_: (b, 0)),
            scratch_shapes=[pltpu.VMEM((snp_rows, 2 * width), jnp.bfloat16)],
        ),
        compiler_params=pltpu.CompilerParams(vmem_limit_bytes=LIMIT),
    )(counts, snps, vectors, scores)


def gram_kernel(counts, slots, weighted, panels, scale, out):
    pair = pl.program_id(0)
    width = weighted.shape[1]
    left = weighted[...].astype(jnp.float32)
    rows = lax.broadcasted_iota(jnp.int32, left.shape, 0)
    first = rows < counts[2 * pair]
    left = jnp.concatenate([jnp.where(first, left, 0.0).T, jnp.where(first, 0.0, left).T], axis=0)
    left = left.astype(jnp.bfloat16)
    shape = (width, width)
    same = lax.broadcasted_iota(jnp.int32, shape, 0) == lax.broadcasted_iota(jnp.int32, shape, 1)
    for index in range(out.shape[0]):
        both = jnp.dot(left, panels[slots[index]], preferred_element_type=jnp.float32)
        for side in range(2):
            gram = both[side * width : (side + 1) * width]
            if index == 0:
                count = counts[2 * pair + side].astype(jnp.float32)
                gram = gram - jnp.where(same, count, 0.0)
            out[index, 0, side] = gram * scale[index]


def grams(weighted, panels, scale, slots, counts):
    blocks = counts.shape[0]
    rounds, width = scale.shape[:2]
    pair_rows = 2 * weighted.shape[0] // blocks
    return pl.pallas_call(
        gram_kernel,
        out_shape=jax.ShapeDtypeStruct((rounds, 1, blocks, width, width), jnp.float32),
        grid_spec=pltpu.PrefetchScalarGridSpec(
            num_scalar_prefetch=2,
            grid=(blocks // 2,),
            in_specs=[
                pl.BlockSpec((pair_rows, width), lambda b, *_: (b, 0)),
                pl.BlockSpec((panels.shape[0], pair_rows, width), lambda b, *_: (0, b, 0)),
                pl.BlockSpec(scale.shape, lambda b, *_: (0, 0, 0)),
            ],
            out_specs=pl.BlockSpec((rounds, 1, 2, width, width), lambda b, *_: (0, 0, b, 0, 0)),
        ),
        compiler_params=pltpu.CompilerParams(vmem_limit_bytes=LIMIT),
    )(counts, slots, weighted, panels, scale)


def exchange_kernel(counts, snps, own, own_values, scores, out, held, values, left, store, masked,
                    here, send1, recv1, send2, recv2, send3, recv3):
    line = lax.axis_size("panel") // 4
    me = lax.axis_index("panel")
    z = me // 4
    y = (me // 2) % 2
    k = me % 2
    piece = own.shape[0]
    pair_rows = 4 * piece
    halves = recv1.shape[1]
    part = piece // halves
    chunks = left.shape[0]
    cuts = recv2.shape[1] // chunks
    units = chunks * cuts
    cut_rows = pair_rows // cuts
    top = line - 1
    up, down, across, beside = me + 4, me - 4, me + 2 - 4 * y, me + 1 - 2 * k
    pending = []

    barrier = pltpu.get_barrier_semaphore()
    others = 4 * line - 1
    for step in range(1, others + 1):
        target = lax.rem(me + step, others + 1)
        pl.semaphore_signal(
            barrier, inc=1, device_id={"panel": target}, device_id_type=pl.DeviceIdType.MESH
        )
    pl.semaphore_wait(barrier, others)

    def start(condition, copy):
        if condition is None:
            copy.start()
        else:
            pl.when(condition)(copy.start)
        pending.append((condition, copy))

    def move1(source, half, way, target, first=False):
        rows = pl.ds(source * piece + half * part, part)
        origin = own.at[pl.ds(half * part, part)] if first else store.at[rows]
        return pltpu.make_async_remote_copy(
            src_ref=origin,
            dst_ref=store.at[rows],
            send_sem=send1.at[way, source, half],
            recv_sem=recv1.at[source, half],
            device_id={"panel": target},
            device_id_type=pl.DeviceIdType.MESH,
        )

    def arrive1(source, half):
        move1(source, half, 0, beside).wait_recv()

    def move2(source, chunk, bit, way, target):
        rows = pl.ds(chunk * pair_rows + bit * cut_rows, cut_rows)
        unit = chunk * cuts + bit
        return pltpu.make_async_remote_copy(
            src_ref=held.at[source, rows],
            dst_ref=held.at[source, rows],
            send_sem=send2.at[way, source, unit],
            recv_sem=recv2.at[source, unit],
            device_id={"panel": target},
            device_id_type=pl.DeviceIdType.MESH,
        )

    def arrive2(source, chunk, bit):
        move2(source, chunk, bit, 0, beside).wait_recv()

    def move3(source, step, target):
        return pltpu.make_async_remote_copy(
            src_ref=own_values,
            dst_ref=values.at[source],
            send_sem=send3.at[step],
            recv_sem=recv3.at[source],
            device_id={"panel": target},
            device_id_type=pl.DeviceIdType.MESH,
        )

    def spread(condition, chunk, bit, source, behind):
        side = (behind >= y) & (behind <= y + 1)
        near = behind <= 2
        start(condition & side, move2(source, chunk, bit, 2, across))
        start(condition & near, move2(source, chunk, bit, 3, beside))

    def order(source, step):
        far = source // 4
        near = jnp.minimum(far, top - far)
        nearest = jnp.where(step > 2 * near, step, (near + (step + 1) // 2 * (1 - 2 * (step % 2))))
        return jnp.where(far > top - far, top - nearest, nearest)

    for half in range(halves):
        start(z < top, move1(me, half, 0, up, True))
        start(z > 0, move1(me, half, 1, down, True))
        start(None, move1(me, half, 2, across, True))
        start(None, move1(me, half, 3, beside, True))
    for step in range(1, others + 1):
        start(None, move3(me, step, lax.rem(me + step, others + 1)))
    local = [
        pltpu.make_async_copy(own, store.at[pl.ds(me * piece, piece)], here.at[0]),
        pltpu.make_async_copy(own_values, values.at[me], here.at[1]),
    ]
    for copy in local:
        copy.start()

    def plane(index):
        rows = pl.ds(index * pair_rows, pair_rows)
        held[me, rows] = project_rows(store[rows], masked[index], counts[2 * index])

    def column(distance):
        for half in range(halves):
            def below():
                arrive1(me - 4 * distance, half)
            def above():
                arrive1(me + 4 * distance, half)
            has_below, has_above = z >= distance, z + distance <= top
            pl.when(has_below)(below)
            source = me - 4 * distance
            start(has_below & (z < top), move1(source, half, 0, up))
            start(has_below, move1(source, half, 2, across))
            start(has_below, move1(source, half, 3, beside))
            pl.when(has_above)(above)
            source = me + 4 * distance
            start(has_above & (z > 0), move1(source, half, 1, down))
            start(has_above, move1(source, half, 2, across))
            start(has_above, move1(source, half, 3, beside))

    def sideways(distance, sign):
        has = (z >= distance) if sign < 0 else (z + distance <= top)
        source = across + sign * 4 * distance
        for half in range(halves):
            pl.when(has)(functools.partial(arrive1, source, half))
            start(has, move1(source, half, 3, beside))

    def finish(distance, sign):
        has = (z >= distance) if sign < 0 else (z + distance <= top)

        @pl.when(has)
        def _():
            for source in (beside, beside + 2 - 4 * y):
                for half in range(halves):
                    arrive1(source + sign * 4 * distance, half)
            plane(z + sign * distance)

        chunk = z + sign * distance
        for bit in range(cuts):
            start(has & (z < top), move2(me, chunk, bit, 0, up))
            start(has & (z >= line - 2), move2(me, chunk, bit, 1, down))
            spread(has, chunk, bit, me, 0)

    for distance in range(1, line + 1):
        if distance < line:
            column(distance)
        if distance == 1:
            for pair in range(line):
                place_masked(snps, scores.at[0, pl.ds(2 * pair, 2)], pair, masked.at[pair])
            for copy in local:
                copy.wait()
        last = distance - 1
        signs = (1,) if last == 0 else (-1, 1)
        for sign in signs:
            sideways(last, sign)
        for sign in signs:
            finish(last, sign)

    cross = []
    for lag in range(2):
        plane_index = lax.rem(z - lag - (1 - y) + line, line)
        cross.append(plane_index * 4 + (1 - y) * 2 + k)
    def weigh(index):
        rows = pl.ds(index * pair_rows, pair_rows)
        row = values[4 * index] + values[4 * index + 1]
        row = row + (values[4 * index + 2] + values[4 * index + 3])
        flat = held[me, rows].astype(jnp.float32).T / row[0:1]
        first = lax.broadcasted_iota(jnp.int32, flat.shape, 1) < counts[2 * index]
        both = jnp.concatenate([jnp.where(first, flat, 0.0), jnp.where(first, 0.0, flat)], axis=0)
        left[index] = both.astype(jnp.bfloat16)

    def gram(source, chunk, number, own_panel=False):
        rows = pl.ds(chunk * pair_rows, pair_rows)
        both = jnp.dot(left[chunk], held[source, rows], preferred_element_type=jnp.float32)
        width = both.shape[1]
        for side in range(2):
            part = both[side * width : (side + 1) * width]
            if own_panel:
                shape = (width, width)
                across_rows = lax.broadcasted_iota(jnp.int32, shape, 0)
                same = across_rows == lax.broadcasted_iota(jnp.int32, shape, 1)
                count = counts[2 * chunk + side].astype(jnp.float32)
                part = part - jnp.where(same, count, 0.0)
            out[number, 0, 2 * chunk + side] = part

    near = [lax.rem(z - lag + line, line) * 4 + y * 2 + k for lag in range(3)]
    swap = 1 - 2 * k

    for unit in range(units + 2):
        step, bit = unit // cuts, unit % cuts
        if unit < units:
            for distance in range(1, line):
                if distance <= 2:
                    has = z >= distance
                    source = me - 4 * distance
                    chunk = order(source, step)
                    pl.when(has)(functools.partial(arrive2, source, chunk, bit))
                    if distance == 1:
                        start(has & (z < top), move2(source, chunk, bit, 0, up))
                    spread(has, chunk, bit, source, distance)
                has = (z + distance <= top) & (z + distance >= line - 2)
                source = me + 4 * distance
                chunk = order(source, step)
                pl.when(has)(functools.partial(arrive2, source, chunk, bit))
                start(has & (z > 0), move2(source, chunk, bit, 1, down))
                spread(has, chunk, bit, source, line - distance)
        if unit == 0:
            for number in range(1, others + 1):
                move3(lax.rem(me + number, others + 1), number, beside).wait_recv()
            for index in range(chunks):
                weigh(index)
        step, bit = (unit - 1) // cuts, (unit - 1) % cuts
        if 0 < unit <= units:
            for source in cross:
                chunk = order(source, step)
                arrive2(source, chunk, bit)
                start(None, move2(source, chunk, bit, 3, beside))
            if bit == cuts - 1:
                for lag, source in enumerate(near):
                    gram(source, order(source, step), 4 * lag, lag == 0)
                for lag, source in enumerate(cross):
                    gram(source, order(source, step), 4 * lag + 2)
        step, bit = (unit - 2) // cuts, (unit - 2) % cuts
        if unit > 1:
            for source in near + cross:
                arrive2(source + swap, order(source, step), bit)
            if bit == cuts - 1:
                for lag, source in enumerate(near):
                    number = 4 * lag - swap

                    @pl.when((number >= 0) & (number < out.shape[0]))
                    def _():
                        gram(source + swap, order(source, step), number)

                for lag, source in enumerate(cross):
                    gram(source + swap, order(source, step), 4 * lag + 2 - swap)
    for condition, copy in pending:
        if condition is None:
            copy.wait_send()
        else:
            pl.when(condition)(copy.wait_send)


def exchange(vectors, values, counts, snps, scores):
    devices = lax.axis_size("panel")
    piece, depth = vectors.shape
    blocks, snp_rows, width = scores.shape[1:]
    row_total = devices * piece
    pair_rows = 4 * piece
    place = lax.rem(lax.axis_index("panel"), 4) * piece
    rider = jnp.zeros((8, pair_rows), jnp.float32)
    spread = jnp.broadcast_to(values.astype(jnp.float32), (8, piece))
    rider = lax.dynamic_update_slice_in_dim(rider, spread, place, 1)
    halves = HALVES
    cuts = CUTS
    chunks = blocks // 2
    vmem = pl.BlockSpec(memory_space=pltpu.VMEM)
    smem = pl.BlockSpec(memory_space=pltpu.SMEM)
    return pl.pallas_call(
        exchange_kernel,
        out_shape=jax.ShapeDtypeStruct((ROUNDS + 1, 1, blocks, width, width), jnp.float32),
        in_specs=[smem, smem, vmem, vmem, vmem],
        out_specs=vmem,
        scratch_shapes=[
            pltpu.VMEM((devices, row_total, width), jnp.bfloat16),
            pltpu.VMEM((devices, 8, pair_rows), jnp.float32),
            pltpu.VMEM((chunks, 2 * width, pair_rows), jnp.bfloat16),
            pltpu.VMEM((row_total, depth), jnp.bfloat16),
            pltpu.VMEM((blocks // 2, snp_rows, 2 * width), jnp.bfloat16),
            pltpu.SemaphoreType.DMA((2,)),
            pltpu.SemaphoreType.DMA((4, devices, halves)),
            pltpu.SemaphoreType.DMA((devices, halves)),
            pltpu.SemaphoreType.DMA((4, devices, chunks * cuts)),
            pltpu.SemaphoreType.DMA((devices, chunks * cuts)),
            pltpu.SemaphoreType.DMA((devices,)),
            pltpu.SemaphoreType.DMA((devices,)),
        ],
        compiler_params=pltpu.CompilerParams(
            collective_id=0, has_side_effects=True, vmem_limit_bytes=LIMIT
        ),
    )(counts, snps, vectors, rider, scores)


def per_device(eig_vectors, eig_values, eig_count, snp_count, zscores, samples):
    devices = lax.axis_size("panel")
    spacing = max(1, devices // 32)
    panels = devices // spacing
    slot_index = lax.axis_index("panel")
    panel_index = slot_index // spacing
    group_index = slot_index % spacing
    blocks_here, snp_rows, panel_width = zscores.shape[1:]
    counts = lax.dynamic_slice_in_dim(eig_count, group_index * blocks_here, blocks_here)
    snps = lax.dynamic_slice_in_dim(snp_count, group_index * blocks_here, blocks_here)
    rounds = jnp.arange(ROUNDS + 1, dtype=jnp.int32)
    partners = (panel_index - rounds) % panels
    scales = samples.astype(jnp.float32).reshape(panels, panel_width)
    own_scale = lax.dynamic_index_in_dim(scales, panel_index, 0, keepdims=False)
    scale = 1.0 / jnp.sqrt(own_scale[None, :, None] * scales[partners][:, None, :])

    if spacing == 1 and panels == 2 * ROUNDS and blocks_here == panels // 2:
        raw = exchange(eig_vectors, eig_values, counts, snps, zscores)
        return raw * scale[:, None, None]
    members = [[g + spacing * i for i in range(panels)] for g in range(spacing)]
    gather = functools.partial(
        lax.all_gather, axis_name="panel", axis_index_groups=members if spacing > 1 else None
    )
    vectors = gather(eig_vectors, tiled=True)
    values = gather(eig_values, tiled=True)
    projected = project(vectors, zscores, counts, snps)
    held = gather(projected)
    weighted = (projected.astype(jnp.float32) / values.astype(jnp.float32)[:, None]).astype(
        jnp.bfloat16
    )
    return grams(weighted, held, scale, partners, counts)


def solution(mesh):
    placed = (
        P(("groups", "panel"), None),
        P(("groups", "panel")),
        P("groups"),
        P("groups"),
        P(("groups", "panel"), None, None, None),
        P("groups"),
    )
    return jax.shard_map(
        per_device,
        mesh=mesh,
        in_specs=placed,
        out_specs=P(None, ("groups", "panel"), None, None, None),
        check_vma=False,
    )
```

```python
import functools

import jax
import jax.numpy as jnp
from jax import lax
from jax.experimental import pallas as pl
from jax.experimental.pallas import tpu as pltpu
from jax.sharding import PartitionSpec as P

ROUNDS = 8
HALVES = 2
CUTS = 2
LIMIT = 56 * 1024 * 1024


def place_masked(snps, scores, pair, store):
    width = scores.shape[-1]
    for side in range(2):
        block = 2 * pair + side
        rows = lax.broadcasted_iota(jnp.int32, scores.shape[-2:], 0)
        part = jnp.where(rows < snps[block], scores[side].astype(jnp.float32), 0.0)
        store[:, side * width : (side + 1) * width] = part.astype(jnp.bfloat16)


def project_rows(vectors, masked, first_count):
    both = jnp.dot(vectors, masked, preferred_element_type=jnp.float32)
    width = both.shape[1] // 2
    rows = lax.broadcasted_iota(jnp.int32, (both.shape[0], width), 0)
    return jnp.where(rows < first_count, both[:, :width], both[:, width:]).astype(jnp.bfloat16)


def project_kernel(counts, snps, vectors, scores, out, masked):
    pair = pl.program_id(0)
    place_masked(snps, scores.at[0], pair, masked)
    out[...] = project_rows(vectors[...], masked[...], counts[2 * pair])


def project(vectors, scores, counts, snps):
    row_total, depth = vectors.shape
    blocks, snp_rows, width = scores.shape[1:]
    pair_rows = 2 * row_total // blocks
    return pl.pallas_call(
        project_kernel,
        out_shape=jax.ShapeDtypeStruct((row_total, width), jnp.bfloat16),
        grid_spec=pltpu.PrefetchScalarGridSpec(
            num_scalar_prefetch=2,
            grid=(blocks // 2,),
            in_specs=[
                pl.BlockSpec((pair_rows, depth), lambda b, *_: (b, 0)),
                pl.BlockSpec((1, 2, snp_rows, width), lambda b, *_: (0, b, 0, 0)),
            ],
            out_specs=pl.BlockSpec((pair_rows, width), lambda b, *_: (b, 0)),
            scratch_shapes=[pltpu.VMEM((snp_rows, 2 * width), jnp.bfloat16)],
        ),
        compiler_params=pltpu.CompilerParams(vmem_limit_bytes=LIMIT),
    )(counts, snps, vectors, scores)


def gram_kernel(counts, slots, weighted, panels, scale, out):
    pair = pl.program_id(0)
    width = weighted.shape[1]
    left = weighted[...].astype(jnp.float32)
    rows = lax.broadcasted_iota(jnp.int32, left.shape, 0)
    first = rows < counts[2 * pair]
    left = jnp.concatenate([jnp.where(first, left, 0.0).T, jnp.where(first, 0.0, left).T], axis=0)
    left = left.astype(jnp.bfloat16)
    shape = (width, width)
    same = lax.broadcasted_iota(jnp.int32, shape, 0) == lax.broadcasted_iota(jnp.int32, shape, 1)
    for index in range(out.shape[0]):
        both = jnp.dot(left, panels[slots[index]], preferred_element_type=jnp.float32)
        for side in range(2):
            gram = both[side * width : (side + 1) * width]
            if index == 0:
                count = counts[2 * pair + side].astype(jnp.float32)
                gram = gram - jnp.where(same, count, 0.0)
            out[index, 0, side] = gram * scale[index]


def grams(weighted, panels, scale, slots, counts):
    blocks = counts.shape[0]
    rounds, width = scale.shape[:2]
    pair_rows = 2 * weighted.shape[0] // blocks
    return pl.pallas_call(
        gram_kernel,
        out_shape=jax.ShapeDtypeStruct((rounds, 1, blocks, width, width), jnp.float32),
        grid_spec=pltpu.PrefetchScalarGridSpec(
            num_scalar_prefetch=2,
            grid=(blocks // 2,),
            in_specs=[
                pl.BlockSpec((pair_rows, width), lambda b, *_: (b, 0)),
                pl.BlockSpec((panels.shape[0], pair_rows, width), lambda b, *_: (0, b, 0)),
                pl.BlockSpec(scale.shape, lambda b, *_: (0, 0, 0)),
            ],
            out_specs=pl.BlockSpec((rounds, 1, 2, width, width), lambda b, *_: (0, 0, b, 0, 0)),
        ),
        compiler_params=pltpu.CompilerParams(vmem_limit_bytes=LIMIT),
    )(counts, slots, weighted, panels, scale)


def exchange_kernel(counts, snps, own, own_values, scores, out, held, values, left, store, masked,
                    here, send1, recv1, send2, recv2, send3, recv3):
    line = lax.axis_size("panel") // 4
    me = lax.axis_index("panel")
    z = me // 4
    y = (me // 2) % 2
    k = me % 2
    piece = own.shape[0]
    pair_rows = 4 * piece
    halves = recv1.shape[1]
    part = piece // halves
    chunks = left.shape[0]
    cuts = recv2.shape[1] // chunks
    units = chunks * cuts
    cut_rows = pair_rows // cuts
    top = line - 1
    up, down, across, beside = me + 4, me - 4, me + 2 - 4 * y, me + 1 - 2 * k
    pending = []

    barrier = pltpu.get_barrier_semaphore()
    others = 4 * line - 1
    for step in range(1, others + 1):
        target = lax.rem(me + step, others + 1)
        pl.semaphore_signal(
            barrier, inc=1, device_id={"panel": target}, device_id_type=pl.DeviceIdType.MESH
        )
    pl.semaphore_wait(barrier, others)

    def start(condition, copy):
        if condition is None:
            copy.start()
        else:
            pl.when(condition)(copy.start)
        pending.append((condition, copy))

    def move1(source, half, way, target, first=False):
        rows = pl.ds(source * piece + half * part, part)
        origin = own.at[pl.ds(half * part, part)] if first else store.at[rows]
        return pltpu.make_async_remote_copy(
            src_ref=origin,
            dst_ref=store.at[rows],
            send_sem=send1.at[way, source, half],
            recv_sem=recv1.at[source, half],
            device_id={"panel": target},
            device_id_type=pl.DeviceIdType.MESH,
        )

    def arrive1(source, half):
        move1(source, half, 0, beside).wait_recv()

    def move2(source, chunk, bit, way, target):
        rows = pl.ds(chunk * pair_rows + bit * cut_rows, cut_rows)
        unit = chunk * cuts + bit
        return pltpu.make_async_remote_copy(
            src_ref=held.at[source, rows],
            dst_ref=held.at[source, rows],
            send_sem=send2.at[way, source, unit],
            recv_sem=recv2.at[source, unit],
            device_id={"panel": target},
            device_id_type=pl.DeviceIdType.MESH,
        )

    def arrive2(source, chunk, bit):
        move2(source, chunk, bit, 0, beside).wait_recv()

    def move3(source, step, target):
        return pltpu.make_async_remote_copy(
            src_ref=own_values,
            dst_ref=values.at[source],
            send_sem=send3.at[step],
            recv_sem=recv3.at[source],
            device_id={"panel": target},
            device_id_type=pl.DeviceIdType.MESH,
        )

    def spread(condition, chunk, bit, source, behind):
        side = (behind >= y) & (behind <= y + 1)
        near = behind <= 2
        start(condition & side, move2(source, chunk, bit, 2, across))
        start(condition & near, move2(source, chunk, bit, 3, beside))

    def order(source, step):
        far = source // 4
        near = jnp.minimum(far, top - far)
        nearest = jnp.where(step > 2 * near, step, (near + (step + 1) // 2 * (1 - 2 * (step % 2))))
        return jnp.where(far > top - far, top - nearest, nearest)

    for half in range(halves):
        start(z < top, move1(me, half, 0, up, True))
        start(z > 0, move1(me, half, 1, down, True))
        start(None, move1(me, half, 2, across, True))
        start(None, move1(me, half, 3, beside, True))
    for step in range(1, others + 1):
        start(None, move3(me, step, lax.rem(me + step, others + 1)))
    local = [
        pltpu.make_async_copy(own, store.at[pl.ds(me * piece, piece)], here.at[0]),
        pltpu.make_async_copy(own_values, values.at[me], here.at[1]),
    ]
    for copy in local:
        copy.start()

    for pair in range(line):
        place_masked(snps, scores.at[0, pl.ds(2 * pair, 2)], pair, masked.at[pair])
    for copy in local:
        copy.wait()

    def plane(index):
        rows = pl.ds(index * pair_rows, pair_rows)
        held[me, rows] = project_rows(store[rows], masked[index], counts[2 * index])

    def column(distance):
        for half in range(halves):
            def below():
                arrive1(me - 4 * distance, half)
            def above():
                arrive1(me + 4 * distance, half)
            has_below, has_above = z >= distance, z + distance <= top
            pl.when(has_below)(below)
            source = me - 4 * distance
            start(has_below & (z < top), move1(source, half, 0, up))
            start(has_below, move1(source, half, 2, across))
            start(has_below, move1(source, half, 3, beside))
            pl.when(has_above)(above)
            source = me + 4 * distance
            start(has_above & (z > 0), move1(source, half, 1, down))
            start(has_above, move1(source, half, 2, across))
            start(has_above, move1(source, half, 3, beside))

    def sideways(distance, sign):
        has = (z >= distance) if sign < 0 else (z + distance <= top)
        source = across + sign * 4 * distance
        for half in range(halves):
            pl.when(has)(functools.partial(arrive1, source, half))
            start(has, move1(source, half, 3, beside))

    def finish(distance, sign):
        has = (z >= distance) if sign < 0 else (z + distance <= top)

        @pl.when(has)
        def _():
            for source in (beside, beside + 2 - 4 * y):
                for half in range(halves):
                    arrive1(source + sign * 4 * distance, half)
            plane(z + sign * distance)

        chunk = z + sign * distance
        for bit in range(cuts):
            start(has & (z < top), move2(me, chunk, bit, 0, up))
            start(has & (z >= line - 2), move2(me, chunk, bit, 1, down))
            spread(has, chunk, bit, me, 0)

    for distance in range(1, line + 1):
        if distance < line:
            column(distance)
        last = distance - 1
        signs = (1,) if last == 0 else (-1, 1)
        for sign in signs:
            sideways(last, sign)
        for sign in signs:
            finish(last, sign)

    cross = []
    for lag in range(2):
        plane_index = lax.rem(z - lag - (1 - y) + line, line)
        cross.append(plane_index * 4 + (1 - y) * 2 + k)
    def weigh(index):
        rows = pl.ds(index * pair_rows, pair_rows)
        row = values[4 * index] + values[4 * index + 1]
        row = row + (values[4 * index + 2] + values[4 * index + 3])
        flat = held[me, rows].astype(jnp.float32).T / row[0:1]
        first = lax.broadcasted_iota(jnp.int32, flat.shape, 1) < counts[2 * index]
        both = jnp.concatenate([jnp.where(first, flat, 0.0), jnp.where(first, 0.0, flat)], axis=0)
        left[index] = both.astype(jnp.bfloat16)

    def gram(source, chunk, number, own_panel=False):
        rows = pl.ds(chunk * pair_rows, pair_rows)
        both = jnp.dot(left[chunk], held[source, rows], preferred_element_type=jnp.float32)
        width = both.shape[1]
        for side in range(2):
            part = both[side * width : (side + 1) * width]
            if own_panel:
                shape = (width, width)
                across_rows = lax.broadcasted_iota(jnp.int32, shape, 0)
                same = across_rows == lax.broadcasted_iota(jnp.int32, shape, 1)
                count = counts[2 * chunk + side].astype(jnp.float32)
                part = part - jnp.where(same, count, 0.0)
            out[number, 0, 2 * chunk + side] = part

    near = [lax.rem(z - lag + line, line) * 4 + y * 2 + k for lag in range(3)]
    swap = 1 - 2 * k

    for unit in range(units + 2):
        step, bit = unit // cuts, unit % cuts
        if unit < units:
            for distance in range(1, line):
                if distance <= 2:
                    has = z >= distance
                    source = me - 4 * distance
                    chunk = order(source, step)
                    pl.when(has)(functools.partial(arrive2, source, chunk, bit))
                    if distance == 1:
                        start(has & (z < top), move2(source, chunk, bit, 0, up))
                    spread(has, chunk, bit, source, distance)
                has = (z + distance <= top) & (z + distance >= line - 2)
                source = me + 4 * distance
                chunk = order(source, step)
                pl.when(has)(functools.partial(arrive2, source, chunk, bit))
                start(has & (z > 0), move2(source, chunk, bit, 1, down))
                spread(has, chunk, bit, source, line - distance)
        if unit == 0:
            for number in range(1, others + 1):
                move3(lax.rem(me + number, others + 1), number, beside).wait_recv()
            for index in range(chunks):
                weigh(index)
        step, bit = (unit - 1) // cuts, (unit - 1) % cuts
        if 0 < unit <= units:
            for source in cross:
                chunk = order(source, step)
                arrive2(source, chunk, bit)
                start(None, move2(source, chunk, bit, 3, beside))
            if bit == cuts - 1:
                for lag, source in enumerate(near):
                    gram(source, order(source, step), 4 * lag, lag == 0)
                for lag, source in enumerate(cross):
                    gram(source, order(source, step), 4 * lag + 2)
        step, bit = (unit - 2) // cuts, (unit - 2) % cuts
        if unit > 1:
            for source in near + cross:
                arrive2(source + swap, order(source, step), bit)
            if bit == cuts - 1:
                for lag, source in enumerate(near):
                    number = 4 * lag - swap

                    @pl.when((number >= 0) & (number < out.shape[0]))
                    def _():
                        gram(source + swap, order(source, step), number)

                for lag, source in enumerate(cross):
                    gram(source + swap, order(source, step), 4 * lag + 2 - swap)
    for condition, copy in pending:
        if condition is None:
            copy.wait_send()
        else:
            pl.when(condition)(copy.wait_send)


def exchange(vectors, values, counts, snps, scores):
    devices = lax.axis_size("panel")
    piece, depth = vectors.shape
    blocks, snp_rows, width = scores.shape[1:]
    row_total = devices * piece
    pair_rows = 4 * piece
    place = lax.rem(lax.axis_index("panel"), 4) * piece
    rider = jnp.zeros((8, pair_rows), jnp.float32)
    spread = jnp.broadcast_to(values.astype(jnp.float32), (8, piece))
    rider = lax.dynamic_update_slice_in_dim(rider, spread, place, 1)
    halves = HALVES
    cuts = CUTS
    chunks = blocks // 2
    vmem = pl.BlockSpec(memory_space=pltpu.VMEM)
    smem = pl.BlockSpec(memory_space=pltpu.SMEM)
    return pl.pallas_call(
        exchange_kernel,
        out_shape=jax.ShapeDtypeStruct((ROUNDS + 1, 1, blocks, width, width), jnp.float32),
        in_specs=[smem, smem, vmem, vmem, vmem],
        out_specs=vmem,
        scratch_shapes=[
            pltpu.VMEM((devices, row_total, width), jnp.bfloat16),
            pltpu.VMEM((devices, 8, pair_rows), jnp.float32),
            pltpu.VMEM((chunks, 2 * width, pair_rows), jnp.bfloat16),
            pltpu.VMEM((row_total, depth), jnp.bfloat16),
            pltpu.VMEM((blocks // 2, snp_rows, 2 * width), jnp.bfloat16),
            pltpu.SemaphoreType.DMA((2,)),
            pltpu.SemaphoreType.DMA((4, devices, halves)),
            pltpu.SemaphoreType.DMA((devices, halves)),
            pltpu.SemaphoreType.DMA((4, devices, chunks * cuts)),
            pltpu.SemaphoreType.DMA((devices, chunks * cuts)),
            pltpu.SemaphoreType.DMA((devices,)),
            pltpu.SemaphoreType.DMA((devices,)),
        ],
        compiler_params=pltpu.CompilerParams(
            collective_id=0, has_side_effects=True, vmem_limit_bytes=LIMIT
        ),
    )(counts, snps, vectors, rider, scores)


def per_device(eig_vectors, eig_values, eig_count, snp_count, zscores, samples):
    devices = lax.axis_size("panel")
    spacing = max(1, devices // 32)
    panels = devices // spacing
    slot_index = lax.axis_index("panel")
    panel_index = slot_index // spacing
    group_index = slot_index % spacing
    blocks_here, snp_rows, panel_width = zscores.shape[1:]
    counts = lax.dynamic_slice_in_dim(eig_count, group_index * blocks_here, blocks_here)
    snps = lax.dynamic_slice_in_dim(snp_count, group_index * blocks_here, blocks_here)
    rounds = jnp.arange(ROUNDS + 1, dtype=jnp.int32)
    partners = (panel_index - rounds) % panels
    scales = samples.astype(jnp.float32).reshape(panels, panel_width)
    own_scale = lax.dynamic_index_in_dim(scales, panel_index, 0, keepdims=False)
    scale = 1.0 / jnp.sqrt(own_scale[None, :, None] * scales[partners][:, None, :])

    if spacing == 1 and panels == 2 * ROUNDS and blocks_here == panels // 2:
        raw = exchange(eig_vectors, eig_values, counts, snps, zscores)
        return raw * scale[:, None, None]
    members = [[g + spacing * i for i in range(panels)] for g in range(spacing)]
    gather = functools.partial(
        lax.all_gather, axis_name="panel", axis_index_groups=members if spacing > 1 else None
    )
    vectors = gather(eig_vectors, tiled=True)
    values = gather(eig_values, tiled=True)
    projected = project(vectors, zscores, counts, snps)
    held = gather(projected)
    weighted = (projected.astype(jnp.float32) / values.astype(jnp.float32)[:, None]).astype(
        jnp.bfloat16
    )
    return grams(weighted, held, scale, partners, counts)


def solution(mesh):
    placed = (
        P(("groups", "panel"), None),
        P(("groups", "panel")),
        P("groups"),
        P("groups"),
        P(("groups", "panel"), None, None, None),
        P("groups"),
    )
    return jax.shard_map(
        per_device,
        mesh=mesh,
        in_specs=placed,
        out_specs=P(None, ("groups", "panel"), None, None, None),
        check_vma=False,
    )
```
